32 devices in a mesh: lon: 8 (over y, x, core), lat: 4 (over z).
Axes of the slice: x: 2, y: 2, z: 4, core: 2. Of those that a mesh axis runs over, the one named last changes fastest.
Arguments:
- first_features: bfloat16 [32, 2048, 128], P(None, ('lon', 'lat')), may hold values from -6 to 6
- second_features: bfloat16 [32, 2048, 128], P(None, ('lon', 'lat')), may hold values from -6 to 6
- hidden_state: bfloat16 [32, 2048, 128], P('lat', 'lon'), may hold values from -1 to 1
- encoder_weight: bfloat16 [289, 128], replicated, may hold values from -0.375 to 0.375
- gates_weight: bfloat16 [3, 3, 256, 256], replicated, may hold values from -0.125 to 0.125
- candidate_weight: bfloat16 [3, 3, 256, 128], replicated, may hold values from -0.125 to 0.125
- row_metric: float32 [32], replicated, may hold values from 1 to 3
Outputs:
- new_state: bfloat16 [32, 2048, 128], P('lat', 'lon')
The draws below stay inside these ranges and needn't reach their ends.
All inputs are finite; a program needn't handle non-finite values.
Results may differ from the reference program's by a relative error of at most 0.0058.
Values may be sent and summed in bfloat16 or wider, within the bound.
A program may use at most 64 MiB of HBM per device.

```python
import math
import jax
import jax.numpy as jnp
from jax import lax

FEAT = 128
HID = 128
MOT = 128
RADIUS = 8
WIN = 17
ROWS = 32
WIDTH = 2048


def levels(key, dims, cuts, smallest, high):
    def one(axis_at, blocks):
        steps = jax.random.uniform(jax.random.fold_in(jax.random.fold_in(key, 6), axis_at), (blocks,), jnp.float32, smallest / len(cuts), high / len(cuts))
        return jnp.repeat(jnp.exp(steps), dims[axis_at] // blocks).reshape((-1,) + (1,) * (len(dims) - axis_at - 1))

    factor_of = one(*cuts[0])
    for cut in cuts[1:]:
        factor_of = factor_of * one(*cut)
    return factor_of


def noise(rng, extent, width, limit, shards=(), kind=jnp.bfloat16):
    entries = jax.random.normal(rng, extent, jnp.float32) * width
    if len(shards) > 0:
        entries = levels(rng, extent, shards, -0.22, 0.18) * entries
    return jnp.clip(entries, min=-limit, max=limit).astype(kind)


def setup_inputs(seed: int = 0) -> dict:
    arg_keys = jax.random.split(jax.random.key(seed), 8)
    first_features = noise(arg_keys[0], (ROWS, WIDTH, FEAT), 1.0, 6.0, ((1, 32),))
    second_features = noise(arg_keys[1], (ROWS, WIDTH, FEAT), 1.0, 6.0, ((1, 32),))
    hidden_state = jnp.clip(jax.random.uniform(arg_keys[2], (ROWS, WIDTH, HID), jnp.float32, -1.0, 1.0) * levels(arg_keys[2], (ROWS, WIDTH, HID), ((0, 4), (1, 8)), -0.4, 0.0), -1.0, 1.0).astype(jnp.bfloat16)
    encoder_weight = noise(arg_keys[3], (WIN * WIN, MOT), (WIN * WIN) ** -0.5, 0.375)
    gates_weight = noise(arg_keys[4], (3, 3, HID + MOT, 2 * HID), (9 * (HID + MOT)) ** -0.5, 0.125)
    candidate_weight = noise(arg_keys[5], (3, 3, HID + MOT, HID), (9 * (HID + MOT)) ** -0.5, 0.125)
    row_metric = jnp.clip(jnp.exp(jax.random.uniform(arg_keys[6], (ROWS,), jnp.float32, math.log(1.0), math.log(3.0))), 1.0, 3.0)
    return {"first_features": first_features, "second_features": second_features, "hidden_state": hidden_state, "encoder_weight": encoder_weight, "gates_weight": gates_weight, "candidate_weight": candidate_weight, "row_metric": row_metric}


def correlate_all(first_map, second_map):
    height = first_map.shape[0]
    columns = first_map.shape[1]
    padded = jnp.pad(second_map, ((RADIUS, RADIUS), (0, 0), (0, 0)))
    padded = jnp.concatenate([padded[:, -RADIUS:], padded, padded[:, :RADIUS]], axis=1)

    def one_row(row_index):
        first_row = lax.dynamic_index_in_dim(first_map, row_index, 0, keepdims=False).astype(jnp.float32)
        strip = lax.dynamic_slice_in_dim(padded, row_index, WIN, 0).astype(jnp.float32)
        planes = []
        for shift_x in range(WIN):
            window = strip[:, shift_x:shift_x + columns]
            planes.append(jnp.einsum("wf,awf->wa", first_row, window, precision=lax.Precision.HIGHEST))
        stacked = jnp.stack(planes, axis=-1)
        return stacked.reshape(columns, WIN * WIN) * (FEAT ** -0.5)

    return lax.map(one_row, jnp.arange(height, dtype=jnp.int32))


def metric_conv(source_map, weights, metric):
    height = source_map.shape[0]
    columns = source_map.shape[1]
    padded = jnp.pad(source_map, ((1, 1), (0, 0), (0, 0)))
    padded = jnp.concatenate([padded[:, -1:], padded, padded[:, :1]], axis=1)
    summed = jnp.zeros((height, columns, weights.shape[-1]), jnp.float32)
    for tap_row in range(3):
        for tap_col in range(3):
            window = padded[tap_row:tap_row + height, tap_col:tap_col + columns].reshape(height * columns, -1)
            contribution = jnp.dot(window, weights[tap_row, tap_col], preferred_element_type=jnp.float32)
            contribution = contribution.reshape(height, columns, -1)
            if tap_col != 1:
                contribution = contribution * metric[:, None, None]
            summed = summed + contribution
    return summed


def reference(first_features, second_features, hidden_state, encoder_weight, gates_weight, candidate_weight, row_metric):
    correlation = correlate_all(first_features, second_features).astype(jnp.bfloat16)
    height = correlation.shape[0]
    columns = correlation.shape[1]
    motion = jax.nn.relu(jnp.dot(correlation.reshape(height * columns, -1), encoder_weight, preferred_element_type=jnp.float32))
    motion = motion.astype(jnp.bfloat16).reshape(height, columns, -1)
    joined = jnp.concatenate([hidden_state, motion], axis=-1)
    gate_values = jax.nn.sigmoid(metric_conv(joined, gates_weight, row_metric))
    update_gate = gate_values[..., :HID]
    reset_gate = gate_values[..., HID:]
    state_float = hidden_state.astype(jnp.float32)
    reset_state = (reset_gate * state_float).astype(jnp.bfloat16)
    candidate = jnp.tanh(metric_conv(jnp.concatenate([reset_state, motion], axis=-1), candidate_weight, row_metric))
    return ((1.0 - update_gate) * state_float + update_gate * candidate).astype(jnp.bfloat16)
```

```python
import functools

import jax
import jax.numpy as jnp
from jax import lax
from jax.experimental import pallas as pl
from jax.experimental.pallas import tpu as pltpu
from jax.sharding import PartitionSpec as P

RADIUS = 8
WIN = 2 * RADIUS + 1
EDGE = 16
LANES = 128
SLOT = 24
PER_GROUP = LANES // SLOT
BF16 = jnp.bfloat16
F32 = jnp.float32


def copy_to(src, dst, sems, slot, lon, lat):
    return pltpu.make_async_remote_copy(
        src_ref=src,
        dst_ref=dst,
        send_sem=sems[0].at[slot],
        recv_sem=sems[1].at[slot],
        device_id={"lon": lon, "lat": lat},
        device_id_type=pl.DeviceIdType.MESH,
    )


def mirror(breadth):
    size = 2 * breadth
    total = lax.broadcasted_iota(jnp.int32, (size, size), 0)
    total += lax.broadcasted_iota(jnp.int32, (size, size), 1)
    return ((total == breadth - 1) | (total == 3 * breadth - 1)).astype(F32).astype(BF16)


def correlate_rows(pair, first, strips, encoder, motion):
    breadth = first.shape[1]
    left = first[pl.ds(2 * pair, 2)].reshape(2 * breadth, first.shape[2])
    groups = -(-WIN // PER_GROUP)
    packed = [[jnp.zeros((breadth, LANES), F32)] * groups for _ in range(2)]
    lane = lax.broadcasted_iota(jnp.int32, (breadth, LANES), 1)
    for step in range(0, WIN + 1, 2):
        right = strips[pl.ds(2 * pair + step, 2)].reshape(2 * LANES, first.shape[2])
        product = lax.dot_general(
            left, right, (((1,), (1,)), ((), ())), preferred_element_type=F32
        )
        for sub in range(2):
            for row in range(2):
                shift_y = step + sub - row
                if not 0 <= shift_y < WIN:
                    continue
                group, place = divmod(shift_y, PER_GROUP)
                band = product[
                    row * breadth : (row + 1) * breadth, sub * LANES : (sub + 1) * LANES
                ]
                start = SLOT * place
                turned = pltpu.roll(
                    band,
                    (start - (EDGE - RADIUS) - (breadth - 1)) % LANES,
                    1,
                    stride=1,
                    stride_axis=0,
                )
                inside = (lane >= start) & (lane < start + WIN)
                packed[row][group] = jnp.where(inside, turned, packed[row][group])
    scale = first.shape[2] ** (-0.5)
    rows = [jnp.concatenate(packed[row], axis=1) for row in range(2)]
    correlation = (jnp.concatenate(rows, axis=0) * scale).astype(BF16)
    out = jnp.dot(correlation, encoder[...], preferred_element_type=F32)
    out = jnp.maximum(out, 0.0).astype(BF16)
    out = jnp.dot(mirror(breadth), out, preferred_element_type=F32).astype(BF16)
    motion[pl.ds(2 * pair + 2, 2)] = out.reshape(2, breadth, -1)


def side_sum(west, east):
    span = west.shape[0]
    return pltpu.roll(west, 1, 0) + pltpu.roll(east, span - 1, 0)


def stacked(field, start, rows):
    span = field.shape[1]
    parts = [field[pl.ds(start + p, rows)].reshape(rows * span, -1) for p in range(3)]
    return parts


def interleave(a, b):
    return jnp.concatenate([part for both in zip(a, b) for part in both], axis=1)


def kernel(
    lats,
    lons,
    metric,
    first_hbm,
    second_hbm,
    hidden_hbm,
    encoder_in,
    gates_hbm,
    cand_hbm,
    out,
    first,
    strips,
    encoder,
    encoder_wide,
    encoder_slots,
    gates_w,
    cand_w,
    motion,
    hid,
    mot,
    reset,
    update,
    local_sems,
    second_sends,
    second_recvs,
    hid_sends,
    hid_recvs,
    mot_sends,
    mot_recvs,
    rim_sends,
    rim_recvs,
    west_recvs,
):
    height, breadth, channels = first.shape
    tile_rows, tile_cols = out.shape[0], out.shape[1]
    span = hid.shape[1]
    lon, lat = lax.axis_index("lon"), lax.axis_index("lat")
    east, west = lax.rem(lon + 1, lons), lax.rem(lon + lons - 1, lons)
    last = lats - 1

    locals_ = [
        (first_hbm, first),
        (second_hbm, strips.at[pl.ds(RADIUS, height), pl.ds(EDGE, breadth)]),
        (hidden_hbm, hid.at[pl.ds(2, tile_rows), pl.ds(EDGE, tile_cols)]),
        (gates_hbm, gates_w),
        (cand_hbm, cand_w),
    ]
    locals_ = [
        pltpu.make_async_copy(src, dst, local_sems.at[i]) for i, (src, dst) in enumerate(locals_)
    ]
    for copy in locals_:
        copy.start()

    zeros = functools.partial(jnp.zeros, dtype=BF16)
    strips[pl.ds(0, RADIUS)] = zeros((RADIUS, LANES, channels))
    strips[pl.ds(RADIUS + height, RADIUS)] = zeros((RADIUS, LANES, channels))
    used = breadth + 2 * EDGE
    if used < LANES:
        strips[pl.ds(RADIUS, height), pl.ds(used, LANES - used)] = zeros(
            (height, LANES - used, channels)
        )
    motion[pl.ds(0, 2)] = zeros((2, breadth, channels))
    motion[pl.ds(2 + height, 2)] = zeros((2, breadth, channels))

    @pl.when(lat == 0)
    def _():
        hid[pl.ds(0, 2)] = zeros((2, span, channels))

    @pl.when(lat == last)
    def _():
        hid[pl.ds(2 + tile_rows, 2)] = zeros((2, span, channels))

    barrier = pltpu.get_barrier_semaphore()
    peers = 0
    for group in (west, lon, east):
        for other in range(lats):
            if group is lon:
                if other == 0:
                    continue
                target = lax.rem(lat + other, lats)
            else:
                target = jnp.int32(other)
            pl.semaphore_signal(
                barrier,
                inc=1,
                device_id={"lon": group, "lat": target},
                device_id_type=pl.DeviceIdType.MESH,
            )
            peers += 1
    pl.semaphore_wait(barrier, peers)

    next_lat, prev_lat = lax.rem(lat + 1, lats), lax.rem(lat + last, lats)
    next_lon = lax.rem(lon + (lat + 1) // lats, lons)
    prev_lon = lax.rem(lon + lons - (lats - lat) // lats, lons)
    seconds = (second_sends, second_recvs)
    second_copies = [
        copy_to(
            second_hbm.at[:, pl.ds(breadth - EDGE, EDGE)],
            strips.at[pl.ds(RADIUS, height), pl.ds(0, EDGE)],
            seconds,
            0,
            next_lon,
            next_lat,
        ),
        copy_to(
            second_hbm.at[:, pl.ds(0, EDGE)],
            strips.at[pl.ds(RADIUS, height), pl.ds(EDGE + breadth, EDGE)],
            seconds,
            1,
            prev_lon,
            prev_lat,
        ),
    ]
    for copy in second_copies:
        copy.start()

    hids = (hid_sends, hid_recvs)
    sides = []
    slot = 0
    for dy in (-1, 0, 1):
        for dx in (-1, 0, 1):
            if dy == 0 and dx == 0:
                continue
            src_rows = {-1: pl.ds(0, 2), 0: pl.ds(0, tile_rows), 1: pl.ds(tile_rows - 2, 2)}[dy]
            dst_rows = {-1: pl.ds(2 + tile_rows, 2), 0: pl.ds(2, tile_rows), 1: pl.ds(0, 2)}[dy]
            src_cols = {
                -1: pl.ds(0, EDGE),
                0: pl.ds(0, tile_cols),
                1: pl.ds(tile_cols - EDGE, EDGE),
            }[dx]
            dst_cols = {
                -1: pl.ds(EDGE + tile_cols, EDGE),
                0: pl.ds(EDGE, tile_cols),
                1: pl.ds(0, EDGE),
            }[dx]
            to_lon = {-1: west, 0: lon, 1: east}[dx]
            to_lat = {-1: prev_lat, 0: lat, 1: next_lat}[dy]
            copy = copy_to(
                hidden_hbm.at[src_rows, src_cols],
                hid.at[dst_rows, dst_cols],
                hids,
                slot,
                to_lon,
                to_lat,
            )
            sends = {-1: lat > 0, 0: None, 1: lat < last}[dy]
            gets = {-1: lat < last, 0: None, 1: lat > 0}[dy]
            sides.append((copy, sends, gets))
            slot += 1

    def maybe(condition, action):
        if condition is None:
            action()
        else:
            pl.when(condition)(action)

    for copy, sends, gets in sides:
        maybe(sends, copy.start)

    encoder_wide[pl.ds(0, WIN * WIN)] = encoder_in[...].astype(F32)
    encoder_slots[...] = jnp.zeros(encoder_slots.shape, F32)
    for shift_y in range(WIN):
        group, place = divmod(shift_y, PER_GROUP)
        piece = encoder_wide[pl.ds(WIN * shift_y, SLOT)]
        row = lax.broadcasted_iota(jnp.int32, piece.shape, 0)
        target = pl.ds(group * LANES + SLOT * place, SLOT)
        encoder_slots[target] = jnp.where(row < WIN, piece, 0.0)
    encoder[...] = encoder_slots[...].astype(BF16)

    locals_[0].wait()

    def reverse(pair, carry):
        rows = first[pl.ds(2 * pair, 2)].reshape(2 * breadth, channels)
        rows = jnp.dot(mirror(breadth), rows, preferred_element_type=F32).astype(BF16)
        first[pl.ds(2 * pair, 2)] = rows.reshape(2, breadth, channels)
        return carry

    lax.fori_loop(0, height // 2, reverse, 0)
    locals_[1].wait()
    for copy in second_copies:
        copy.wait_recv()

    block = tile_rows + 4
    mots = (mot_sends, mot_recvs)
    rims = (rim_sends, rim_recvs)
    wests = (rim_sends, west_recvs)

    def slab_copy(dest):
        return pltpu.make_async_remote_copy(
            src_ref=motion.at[pl.ds(dest * tile_rows, block)],
            dst_ref=mot.at[:, pl.ds(pl.multiple_of(EDGE + lat * breadth, EDGE), breadth)],
            send_sem=mot_sends.at[dest],
            recv_sem=mot_recvs.at[lat],
            device_id={"lon": lon, "lat": jnp.int32(dest)},
            device_id_type=pl.DeviceIdType.MESH,
        )

    def own_copy(dest):
        return pltpu.make_async_copy(
            motion.at[pl.ds(dest * tile_rows, block)],
            mot.at[:, pl.ds(pl.multiple_of(EDGE + lat * breadth, EDGE), breadth)],
            mot_sends.at[dest],
        )

    def west_copy(dest):
        return pltpu.make_async_remote_copy(
            src_ref=motion.at[pl.ds(dest * tile_rows, block), pl.ds(0, EDGE)],
            dst_ref=mot.at[:, pl.ds(EDGE + tile_cols, EDGE)],
            send_sem=rim_sends.at[dest],
            recv_sem=rim_recvs.at[0],
            device_id={"lon": west, "lat": jnp.int32(dest)},
            device_id_type=pl.DeviceIdType.MESH,
        )

    def east_copy(dest):
        return pltpu.make_async_remote_copy(
            src_ref=motion.at[pl.ds(dest * tile_rows, block), pl.ds(breadth - EDGE, EDGE)],
            dst_ref=mot.at[:, pl.ds(0, EDGE)],
            send_sem=rim_sends.at[lats + dest],
            recv_sem=rim_recvs.at[1],
            device_id={"lon": east, "lat": jnp.int32(dest)},
            device_id_type=pl.DeviceIdType.MESH,
        )

    done = 0
    for dest in range(lats):
        upto = min(height, (dest + 1) * tile_rows + 2) // 2

        def step(pair, carry):
            correlate_rows(pair, first, strips, encoder, motion)
            return carry

        lax.fori_loop(done, upto, step, 0)
        done = upto
        maybe(lat == 0, west_copy(dest).start)
        maybe(lat == last, east_copy(dest).start)
        maybe(lat != dest, slab_copy(dest).start)
        maybe(lat == dest, own_copy(dest).start)

    locals_[2].wait()
    locals_[3].wait()
    locals_[4].wait()
    for copy, sends, gets in sides:
        maybe(gets, copy.wait_recv)

    for source in range(lats):
        arrived = pltpu.make_async_remote_copy(
            src_ref=motion.at[pl.ds(0, block)],
            dst_ref=mot.at[:, pl.ds(EDGE + source * breadth, breadth)],
            send_sem=mot_sends.at[source],
            recv_sem=mot_recvs.at[source],
            device_id={"lon": lon, "lat": jnp.int32(source)},
            device_id_type=pl.DeviceIdType.MESH,
        )
        maybe(lat != source, arrived.wait_recv)
        maybe(lat == source, own_copy(source).wait)
    west_copy(0).wait_recv()
    east_copy(0).wait_recv()

    def gate_rows(pair, carry):
        joined = interleave(stacked(hid, 2 * pair, 2), stacked(mot, 2 * pair, 2))
        sums = [
            jnp.dot(joined, gates_w[:, q].reshape(joined.shape[1], -1), preferred_element_type=F32)
            for q in range(3)
        ]
        for row in range(2):
            a, b, c = [s[row * span : (row + 1) * span] for s in sums]
            index = lax.rem(lat * tile_rows + 2 * pair + row + height - 1, height)
            values = jax.nn.sigmoid(b + side_sum(a, c) * metric[index])
            state = hid[2 * pair + row + 1].astype(F32)
            update[2 * pair + row] = values[:, :channels]
            reset[2 * pair + row] = (values[:, channels:] * state).astype(BF16)
        return carry

    lax.fori_loop(0, (tile_rows + 2) // 2, gate_rows, 0)

    def candidate_rows(pair, carry):
        joined = interleave(stacked(reset, 2 * pair, 2), stacked(mot, 2 * pair + 1, 2))
        weights = jnp.concatenate(
            [cand_w[:, q].reshape(joined.shape[1], -1) for q in range(3)], axis=1
        )
        sums = jnp.dot(joined, weights, preferred_element_type=F32)
        for row in range(2):
            part = sums[row * span : (row + 1) * span]
            a, b, c = [part[:, q * channels : (q + 1) * channels] for q in range(3)]
            index = lat * tile_rows + 2 * pair + row
            candidate = jnp.tanh(b + side_sum(a, c) * metric[index])
            gate = update[2 * pair + row + 1]
            state = hid[2 * pair + row + 2].astype(F32)
            new = (1.0 - gate) * state + gate * candidate
            out[2 * pair + row] = new[EDGE : EDGE + tile_cols].astype(BF16)
        return carry

    lax.fori_loop(0, tile_rows // 2, candidate_rows, 0)

    for copy in second_copies:
        copy.wait_send()
    for copy, sends, gets in sides:
        maybe(sends, copy.wait_send)
    for dest in range(lats):
        maybe(lat != dest, slab_copy(dest).wait_send)
        maybe(lat == 0, west_copy(dest).wait_send)
        maybe(lat == last, east_copy(dest).wait_send)


def body(lats, lons, first, second, hidden, encoder, gates, cand, row_metric):
    height, breadth, channels = first.shape
    tile_rows, tile_cols = hidden.shape[:2]
    span = tile_cols + 2 * EDGE
    groups = -(-WIN // PER_GROUP)
    hbm = pl.BlockSpec(memory_space=pl.ANY)
    vmem = pl.BlockSpec(memory_space=pltpu.VMEM)
    dma = pltpu.SemaphoreType.DMA
    return pl.pallas_call(
        functools.partial(kernel, lats, lons),
        out_shape=jax.ShapeDtypeStruct(hidden.shape, hidden.dtype),
        in_specs=[
            pl.BlockSpec(memory_space=pltpu.SMEM),
            hbm,
            hbm,
            hbm,
            vmem,
            hbm,
            hbm,
        ],
        out_specs=vmem,
        scratch_shapes=[
            pltpu.VMEM(first.shape, BF16),
            pltpu.VMEM((height + 2 * RADIUS, LANES, channels), BF16),
            pltpu.VMEM((groups * LANES, encoder.shape[1]), BF16),
            pltpu.VMEM((groups * LANES, encoder.shape[1]), F32),
            pltpu.VMEM((groups * LANES, encoder.shape[1]), F32),
            pltpu.VMEM(gates.shape, BF16),
            pltpu.VMEM(cand.shape, BF16),
            pltpu.VMEM((height + 4, breadth, channels), BF16),
            pltpu.VMEM((tile_rows + 4, span, channels), BF16),
            pltpu.VMEM((tile_rows + 4, span, channels), BF16),
            pltpu.VMEM((tile_rows + 2, span, channels), BF16),
            pltpu.VMEM((tile_rows + 2, span, channels), F32),
            dma((5,)),
            dma((2,)),
            dma((2,)),
            dma((8,)),
            dma((8,)),
            dma((lats,)),
            dma((lats,)),
            dma((2 * lats,)),
            dma((2,)),
            dma((2,)),
        ],
        compiler_params=pltpu.CompilerParams(
            collective_id=0, has_side_effects=True, vmem_limit_bytes=60 * 1024 * 1024
        ),
    )(row_metric, first, second, hidden, encoder, gates, cand)


def solution(mesh):
    return jax.shard_map(
        functools.partial(body, mesh.shape["lat"], mesh.shape["lon"]),
        mesh=mesh,
        in_specs=(
            P(None, ("lon", "lat"), None),
            P(None, ("lon", "lat"), None),
            P("lat", "lon", None),
            P(),
            P(),
            P(),
            P(),
        ),
        out_specs=P("lat", "lon", None),
        check_vma=False,
    )
```

```python
import functools

import jax
import jax.numpy as jnp
from jax import lax
from jax.experimental import pallas as pl
from jax.experimental.pallas import tpu as pltpu
from jax.sharding import PartitionSpec as P

RADIUS = 8
WIN = 2 * RADIUS + 1
EDGE = 16
HALO = 8
LANES = 128
SLOT = 24
PER_GROUP = LANES // SLOT
BF16 = jnp.bfloat16
F32 = jnp.float32


def copy_to(src, dst, sems, slot, lon, lat):
    return pltpu.make_async_remote_copy(
        src_ref=src,
        dst_ref=dst,
        send_sem=sems[0].at[slot],
        recv_sem=sems[1].at[slot],
        device_id={"lon": lon, "lat": lat},
        device_id_type=pl.DeviceIdType.MESH,
    )


def mirror(breadth):
    size = 2 * breadth
    total = lax.broadcasted_iota(jnp.int32, (size, size), 0)
    total += lax.broadcasted_iota(jnp.int32, (size, size), 1)
    return ((total == breadth - 1) | (total == 3 * breadth - 1)).astype(F32).astype(BF16)


def correlate_rows(pair, first, strips, encoder, motion):
    breadth = first.shape[1]
    left = first[pl.ds(2 * pair, 2)].reshape(2 * breadth, first.shape[2])
    groups = -(-WIN // PER_GROUP)
    packed = [[jnp.zeros((breadth, LANES), F32)] * groups for _ in range(2)]
    lane = lax.broadcasted_iota(jnp.int32, (breadth, LANES), 1)
    for step in range(0, WIN + 1, 2):
        right = strips[pl.ds(2 * pair + step, 2)].reshape(2 * LANES, first.shape[2])
        product = lax.dot_general(
            left, right, (((1,), (1,)), ((), ())), preferred_element_type=F32
        )
        for sub in range(2):
            for row in range(2):
                shift_y = step + sub - row
                if not 0 <= shift_y < WIN:
                    continue
                group, place = divmod(shift_y, PER_GROUP)
                band = product[
                    row * breadth : (row + 1) * breadth, sub * LANES : (sub + 1) * LANES
                ]
                start = SLOT * place
                turned = pltpu.roll(
                    band,
                    (start - (EDGE - RADIUS) - (breadth - 1)) % LANES,
                    1,
                    stride=1,
                    stride_axis=0,
                )
                inside = (lane >= start) & (lane < start + WIN)
                packed[row][group] = jnp.where(inside, turned, packed[row][group])
    scale = first.shape[2] ** (-0.5)
    rows = [jnp.concatenate(packed[row], axis=1) for row in range(2)]
    correlation = (jnp.concatenate(rows, axis=0) * scale).astype(BF16)
    out = jnp.dot(correlation, encoder[...], preferred_element_type=F32)
    out = jnp.maximum(out, 0.0).astype(BF16)
    out = jnp.dot(mirror(breadth), out, preferred_element_type=F32).astype(BF16)
    motion[pl.ds(2 * pair, 2)] = out.reshape(2, breadth, -1)


def side_sum(west, east):
    span = west.shape[0]
    return pltpu.roll(west, 1, 0) + pltpu.roll(east, span - 1, 0)


def stacked(field, start, rows):
    span = field.shape[1]
    parts = [field[pl.ds(start + p, rows)].reshape(rows * span, -1) for p in range(3)]
    return parts


def interleave(a, b):
    return jnp.concatenate([part for both in zip(a, b) for part in both], axis=1)


def kernel(
    lats,
    lons,
    metric,
    first_hbm,
    second_hbm,
    hidden_hbm,
    encoder_in,
    gates_hbm,
    cand_hbm,
    out,
    first,
    strips,
    encoder,
    encoder_wide,
    encoder_slots,
    gates_w,
    cand_w,
    motion,
    hid,
    mot,
    reset,
    update,
    state_sums,
    local_sems,
    second_sends,
    second_recvs,
    hid_sends,
    hid_recvs,
    mot_sends,
    mot_recvs,
    rim_sends,
    rim_recvs,
):
    height, breadth, channels = first.shape
    tile_rows, tile_cols = out.shape[0], out.shape[1]
    span = hid.shape[1]
    lon, lat = lax.axis_index("lon"), lax.axis_index("lat")
    east, west = lax.rem(lon + 1, lons), lax.rem(lon + lons - 1, lons)
    last = lats - 1

    locals_ = [
        (first_hbm, first),
        (second_hbm, strips.at[pl.ds(RADIUS, height), pl.ds(EDGE, breadth)]),
        (hidden_hbm, hid.at[pl.ds(2, tile_rows), pl.ds(EDGE, tile_cols)]),
        (gates_hbm, gates_w),
        (cand_hbm, cand_w),
    ]
    locals_ = [
        pltpu.make_async_copy(src, dst, local_sems.at[i]) for i, (src, dst) in enumerate(locals_)
    ]
    for copy in locals_:
        copy.start()

    zeros = functools.partial(jnp.zeros, dtype=BF16)
    strips[pl.ds(0, RADIUS)] = zeros((RADIUS, LANES, channels))
    strips[pl.ds(RADIUS + height, RADIUS)] = zeros((RADIUS, LANES, channels))
    used = breadth + EDGE + HALO
    if used < LANES:
        strips[pl.ds(RADIUS, height), pl.ds(used, LANES - used)] = zeros(
            (height, LANES - used, channels)
        )

    @pl.when(lat == 0)
    def _():
        hid[pl.ds(0, 2)] = zeros((2, span, channels))
        mot[pl.ds(0, 2)] = zeros((2, span, channels))

    @pl.when(lat == last)
    def _():
        hid[pl.ds(2 + tile_rows, 2)] = zeros((2, span, channels))
        mot[pl.ds(2 + tile_rows, 2)] = zeros((2, span, channels))

    barrier = pltpu.get_barrier_semaphore()
    peers = 0
    for group in (west, lon, east):
        for other in range(lats):
            if group is lon:
                if other == 0:
                    continue
                target = lax.rem(lat + other, lats)
            else:
                target = jnp.int32(other)
            pl.semaphore_signal(
                barrier,
                inc=1,
                device_id={"lon": group, "lat": target},
                device_id_type=pl.DeviceIdType.MESH,
            )
            peers += 1
    pl.semaphore_wait(barrier, peers)

    next_lat, prev_lat = lax.rem(lat + 1, lats), lax.rem(lat + last, lats)
    next_lon = lax.rem(lon + (lat + 1) // lats, lons)
    prev_lon = lax.rem(lon + lons - (lats - lat) // lats, lons)
    seconds = (second_sends, second_recvs)
    second_copies = [
        copy_to(
            second_hbm.at[:, pl.ds(breadth - HALO, HALO)],
            strips.at[pl.ds(RADIUS, height), pl.ds(EDGE - HALO, HALO)],
            seconds,
            0,
            next_lon,
            next_lat,
        ),
        copy_to(
            second_hbm.at[:, pl.ds(0, HALO)],
            strips.at[pl.ds(RADIUS, height), pl.ds(EDGE + breadth, HALO)],
            seconds,
            1,
            prev_lon,
            prev_lat,
        ),
    ]
    for copy in second_copies:
        copy.start()

    hids = (hid_sends, hid_recvs)
    sides = []
    slot = 0
    for dy in (-1, 0, 1):
        for dx in (-1, 0, 1):
            if dy == 0 and dx == 0:
                continue
            src_rows = {-1: pl.ds(0, 2), 0: pl.ds(0, tile_rows), 1: pl.ds(tile_rows - 2, 2)}[dy]
            dst_rows = {-1: pl.ds(2 + tile_rows, 2), 0: pl.ds(2, tile_rows), 1: pl.ds(0, 2)}[dy]
            src_cols = {
                -1: pl.ds(0, HALO),
                0: pl.ds(0, tile_cols),
                1: pl.ds(tile_cols - HALO, HALO),
            }[dx]
            dst_cols = {
                -1: pl.ds(EDGE + tile_cols, HALO),
                0: pl.ds(EDGE, tile_cols),
                1: pl.ds(EDGE - HALO, HALO),
            }[dx]
            to_lon = {-1: west, 0: lon, 1: east}[dx]
            to_lat = {-1: prev_lat, 0: lat, 1: next_lat}[dy]
            copy = copy_to(
                hidden_hbm.at[src_rows, src_cols],
                hid.at[dst_rows, dst_cols],
                hids,
                slot,
                to_lon,
                to_lat,
            )
            sends = {-1: lat > 0, 0: None, 1: lat < last}[dy]
            gets = {-1: lat < last, 0: None, 1: lat > 0}[dy]
            sides.append((copy, sends, gets))
            slot += 1

    def maybe(condition, action):
        if condition is None:
            action()
        else:
            pl.when(condition)(action)

    encoder_wide[pl.ds(0, WIN * WIN)] = encoder_in[...].astype(F32)
    encoder_slots[...] = jnp.zeros(encoder_slots.shape, F32)
    for shift_y in range(WIN):
        group, place = divmod(shift_y, PER_GROUP)
        piece = encoder_wide[pl.ds(WIN * shift_y, SLOT)]
        row = lax.broadcasted_iota(jnp.int32, piece.shape, 0)
        target = pl.ds(group * LANES + SLOT * place, SLOT)
        encoder_slots[target] = jnp.where(row < WIN, piece, 0.0)
    encoder[...] = encoder_slots[...].astype(BF16)

    locals_[0].wait()

    def reverse(pair, carry):
        rows = first[pl.ds(2 * pair, 2)].reshape(2 * breadth, channels)
        rows = jnp.dot(mirror(breadth), rows, preferred_element_type=F32).astype(BF16)
        first[pl.ds(2 * pair, 2)] = rows.reshape(2, breadth, channels)
        return carry

    lax.fori_loop(0, height // 2, reverse, 0)
    locals_[1].wait()
    for copy in second_copies:
        copy.wait_recv()
    for copy, sends, gets in sides:
        maybe(sends, copy.start)

    block = tile_rows + 4
    flip = 1 - (2 * lat) // lats
    slab_cols = pl.ds(pl.multiple_of(EDGE + lat * breadth, EDGE), breadth)

    def blocks(dest):
        top = dest * tile_rows
        return [
            (dest == 0, pl.ds(top, block - 2), pl.ds(2, block - 2)),
            ((dest > 0) & (dest < last), pl.ds(top - 2, block), pl.ds(0, block)),
            (dest == last, pl.ds(top - 2, block - 2), pl.ds(0, block - 2)),
        ]

    def slab_copy(dest, source, src_rows, dst_rows):
        cols = pl.ds(pl.multiple_of(EDGE + source * breadth, EDGE), breadth)
        return pltpu.make_async_remote_copy(
            src_ref=motion.at[src_rows],
            dst_ref=mot.at[dst_rows, cols],
            send_sem=mot_sends.at[dest],
            recv_sem=mot_recvs.at[source],
            device_id={"lon": lon, "lat": dest},
            device_id_type=pl.DeviceIdType.MESH,
        )

    def own_copy(src_rows, dst_rows):
        return pltpu.make_async_copy(
            motion.at[src_rows], mot.at[dst_rows, slab_cols], mot_sends.at[lat]
        )

    def west_copy(dest, src_rows, dst_rows):
        return pltpu.make_async_remote_copy(
            src_ref=motion.at[src_rows, pl.ds(0, HALO)],
            dst_ref=mot.at[dst_rows, pl.ds(EDGE + tile_cols, HALO)],
            send_sem=rim_sends.at[dest],
            recv_sem=rim_recvs.at[0],
            device_id={"lon": west, "lat": dest},
            device_id_type=pl.DeviceIdType.MESH,
        )

    def east_copy(dest, src_rows, dst_rows):
        return pltpu.make_async_remote_copy(
            src_ref=motion.at[src_rows, pl.ds(breadth - HALO, HALO)],
            dst_ref=mot.at[dst_rows, pl.ds(EDGE - HALO, HALO)],
            send_sem=rim_sends.at[lats + dest],
            recv_sem=rim_recvs.at[1],
            device_id={"lon": east, "lat": dest},
            device_id_type=pl.DeviceIdType.MESH,
        )

    pairs = height // 2

    def step(index, carry):
        pair = flip * (pairs - 1 - index) + (1 - flip) * index
        correlate_rows(pair, first, strips, encoder, motion)
        return carry

    done = 0
    for turn in range(lats):
        upto = min(height, (turn + 1) * tile_rows + 2) // 2
        lax.fori_loop(done, upto, step, 0)
        done = upto
        dest = flip * (last - turn) + (1 - flip) * turn
        for here, src_rows, dst_rows in blocks(dest):
            maybe(here & (lat != dest), slab_copy(dest, lat, src_rows, dst_rows).start)
            maybe(here & (lat == dest), own_copy(src_rows, dst_rows).start)
            maybe(here & (lat == 0), west_copy(dest, src_rows, dst_rows).start)
            maybe(here & (lat == last), east_copy(dest, src_rows, dst_rows).start)

    locals_[2].wait()
    locals_[3].wait()
    locals_[4].wait()
    for copy, sends, gets in sides:
        maybe(gets, copy.wait_recv)

    def state_rows(pair, carry):
        fields = jnp.concatenate(stacked(hid, 2 * pair, 2), axis=1)
        for q in range(3):
            weights = gates_w[:, q, :channels].reshape(fields.shape[1], -1)
            sums = jnp.dot(fields, weights, preferred_element_type=F32)
            state_sums[q, pl.ds(2 * pair, 2)] = sums.reshape(2, span, -1)
        return carry

    lax.fori_loop(0, (tile_rows + 2) // 2, state_rows, 0)

    for here, src_rows, dst_rows in blocks(lat):
        for source in range(lats):
            arrived = slab_copy(lat, jnp.int32(source), src_rows, dst_rows)
            maybe(here & (lat != source), arrived.wait_recv)
        maybe(here, own_copy(src_rows, dst_rows).wait)
        maybe(here, west_copy(lat, src_rows, dst_rows).wait_recv)
        maybe(here, east_copy(lat, src_rows, dst_rows).wait_recv)

    def gate_rows(pair, carry):
        fields = jnp.concatenate(stacked(mot, 2 * pair, 2), axis=1)
        sums = []
        for q in range(3):
            weights = gates_w[:, q, channels:].reshape(fields.shape[1], -1)
            own = jnp.dot(fields, weights, preferred_element_type=F32)
            sums.append(own.reshape(2, span, -1) + state_sums[q, pl.ds(2 * pair, 2)])
        for row in range(2):
            a, b, c = [s[row] for s in sums]
            index = lax.rem(lat * tile_rows + 2 * pair + row + height - 1, height)
            values = jax.nn.sigmoid(b + side_sum(a, c) * metric[index])
            state = hid[2 * pair + row + 1].astype(F32)
            update[2 * pair + row] = values[:, :channels]
            reset[2 * pair + row] = (values[:, channels:] * state).astype(BF16)
        return carry

    lax.fori_loop(0, (tile_rows + 2) // 2, gate_rows, 0)

    def candidate_rows(pair, carry):
        joined = interleave(stacked(reset, 2 * pair, 2), stacked(mot, 2 * pair + 1, 2))
        weights = jnp.concatenate(
            [cand_w[:, q].reshape(joined.shape[1], -1) for q in range(3)], axis=1
        )
        sums = jnp.dot(joined, weights, preferred_element_type=F32)
        for row in range(2):
            part = sums[row * span : (row + 1) * span]
            a, b, c = [part[:, q * channels : (q + 1) * channels] for q in range(3)]
            index = lat * tile_rows + 2 * pair + row
            candidate = jnp.tanh(b + side_sum(a, c) * metric[index])
            gate = update[2 * pair + row + 1]
            state = hid[2 * pair + row + 2].astype(F32)
            new = (1.0 - gate) * state + gate * candidate
            out[2 * pair + row] = new[EDGE : EDGE + tile_cols].astype(BF16)
        return carry

    lax.fori_loop(0, tile_rows // 2, candidate_rows, 0)

    for copy in second_copies:
        copy.wait_send()
    for copy, sends, gets in sides:
        maybe(sends, copy.wait_send)
    for dest in range(lats):
        dest = jnp.int32(dest)
        for here, src_rows, dst_rows in blocks(dest):
            maybe(here & (lat != dest), slab_copy(dest, lat, src_rows, dst_rows).wait_send)
            maybe(here & (lat == 0), west_copy(dest, src_rows, dst_rows).wait_send)
            maybe(here & (lat == last), east_copy(dest, src_rows, dst_rows).wait_send)


def body(lats, lons, first, second, hidden, encoder, gates, cand, row_metric):
    height, breadth, channels = first.shape
    tile_rows, tile_cols = hidden.shape[:2]
    span = tile_cols + 2 * EDGE
    groups = -(-WIN // PER_GROUP)
    hbm = pl.BlockSpec(memory_space=pl.ANY)
    vmem = pl.BlockSpec(memory_space=pltpu.VMEM)
    dma = pltpu.SemaphoreType.DMA
    return pl.pallas_call(
        functools.partial(kernel, lats, lons),
        out_shape=jax.ShapeDtypeStruct(hidden.shape, hidden.dtype),
        in_specs=[
            pl.BlockSpec(memory_space=pltpu.SMEM),
            hbm,
            hbm,
            hbm,
            vmem,
            hbm,
            hbm,
        ],
        out_specs=vmem,
        scratch_shapes=[
            pltpu.VMEM(first.shape, BF16),
            pltpu.VMEM((height + 2 * RADIUS, LANES, channels), BF16),
            pltpu.VMEM((groups * LANES, encoder.shape[1]), BF16),
            pltpu.VMEM((groups * LANES, encoder.shape[1]), F32),
            pltpu.VMEM((groups * LANES, encoder.shape[1]), F32),
            pltpu.VMEM(gates.shape, BF16),
            pltpu.VMEM(cand.shape, BF16),
            pltpu.VMEM((height, breadth, channels), BF16),
            pltpu.VMEM((tile_rows + 4, span, channels), BF16),
            pltpu.VMEM((tile_rows + 4, span, channels), BF16),
            pltpu.VMEM((tile_rows + 2, span, channels), BF16),
            pltpu.VMEM((tile_rows + 2, span, channels), F32),
            pltpu.VMEM((3, tile_rows + 2, span, gates.shape[-1]), F32),
            dma((5,)),
            dma((2,)),
            dma((2,)),
            dma((8,)),
            dma((8,)),
            dma((lats,)),
            dma((lats,)),
            dma((2 * lats,)),
            dma((2,)),
        ],
        compiler_params=pltpu.CompilerParams(
            collective_id=0, has_side_effects=True, vmem_limit_bytes=60 * 1024 * 1024
        ),
    )(row_metric, first, second, hidden, encoder, gates, cand)


def solution(mesh):
    return jax.shard_map(
        functools.partial(body, mesh.shape["lat"], mesh.shape["lon"]),
        mesh=mesh,
        in_specs=(
            P(None, ("lon", "lat"), None),
            P(None, ("lon", "lat"), None),
            P("lat", "lon", None),
            P(),
            P(),
            P(),
            P(),
        ),
        out_specs=P("lat", "lon", None),
        check_vma=False,
    )
```

```python
import functools

import jax
import jax.numpy as jnp
from jax import lax
from jax.experimental import pallas as pl
from jax.experimental.pallas import tpu as pltpu
from jax.sharding import PartitionSpec as P

RADIUS = 8
WIN = 2 * RADIUS + 1
EDGE = 16
HALO = 8
LANES = 128
SLOT = 24
PER_GROUP = LANES // SLOT
BF16 = jnp.bfloat16
F32 = jnp.float32


def copy_to(src, dst, sems, slot, lon, lat):
    return pltpu.make_async_remote_copy(
        src_ref=src,
        dst_ref=dst,
        send_sem=sems[0].at[slot],
        recv_sem=sems[1].at[slot],
        device_id={"lon": lon, "lat": lat},
        device_id_type=pl.DeviceIdType.MESH,
    )


def mirror(breadth):
    size = 2 * breadth
    total = lax.broadcasted_iota(jnp.int32, (size, size), 0)
    total += lax.broadcasted_iota(jnp.int32, (size, size), 1)
    return ((total == breadth - 1) | (total == 3 * breadth - 1)).astype(F32).astype(BF16)


def correlate_rows(pair, first, strips, encoder, motion):
    breadth = first.shape[1]
    left = first[pl.ds(2 * pair, 2)].reshape(2 * breadth, first.shape[2])
    groups = -(-WIN // PER_GROUP)
    packed = [[jnp.zeros((breadth, LANES), F32)] * groups for _ in range(2)]
    lane = lax.broadcasted_iota(jnp.int32, (breadth, LANES), 1)
    for step in range(0, WIN + 1, 2):
        right = strips[pl.ds(2 * pair + step, 2)].reshape(2 * LANES, first.shape[2])
        product = lax.dot_general(
            left, right, (((1,), (1,)), ((), ())), preferred_element_type=F32
        )
        for sub in range(2):
            for row in range(2):
                shift_y = step + sub - row
                if not 0 <= shift_y < WIN:
                    continue
                group, place = divmod(shift_y, PER_GROUP)
                band = product[
                    row * breadth : (row + 1) * breadth, sub * LANES : (sub + 1) * LANES
                ]
                start = SLOT * place
                turned = pltpu.roll(
                    band,
                    (start - (EDGE - RADIUS) - (breadth - 1)) % LANES,
                    1,
                    stride=1,
                    stride_axis=0,
                )
                inside = (lane >= start) & (lane < start + WIN)
                packed[row][group] = jnp.where(inside, turned, packed[row][group])
    scale = first.shape[2] ** (-0.5)
    rows = [jnp.concatenate(packed[row], axis=1) for row in range(2)]
    correlation = (jnp.concatenate(rows, axis=0) * scale).astype(BF16)
    out = jnp.dot(correlation, encoder[...], preferred_element_type=F32)
    out = jnp.maximum(out, 0.0).astype(BF16)
    out = jnp.dot(mirror(breadth), out, preferred_element_type=F32).astype(BF16)
    motion[pl.ds(2 * pair, 2)] = out.reshape(2, breadth, -1)


def side_sum(west, east):
    span = west.shape[0]
    return pltpu.roll(west, 1, 0) + pltpu.roll(east, span - 1, 0)


def stacked(field, start, rows):
    span = field.shape[1]
    parts = [field[pl.ds(start + p, rows)].reshape(rows * span, -1) for p in range(3)]
    return parts


def kernel(
    lats,
    lons,
    metric,
    first_hbm,
    second_hbm,
    hidden_hbm,
    encoder_in,
    gates_hbm,
    cand_hbm,
    out,
    first,
    strips,
    encoder,
    encoder_wide,
    encoder_slots,
    gates_w,
    cand_w,
    motion,
    hid,
    mot,
    reset,
    update,
    state_sums,
    cand_sums,
    local_sems,
    second_sends,
    second_recvs,
    hid_sends,
    hid_recvs,
    mot_sends,
    mot_recvs,
    rim_sends,
    rim_recvs,
):
    height, breadth, channels = first.shape
    tile_rows, tile_cols = out.shape[0], out.shape[1]
    span = hid.shape[1]
    lon, lat = lax.axis_index("lon"), lax.axis_index("lat")
    east, west = lax.rem(lon + 1, lons), lax.rem(lon + lons - 1, lons)
    last = lats - 1

    locals_ = [
        (first_hbm, first),
        (second_hbm, strips.at[pl.ds(RADIUS, height), pl.ds(EDGE, breadth)]),
        (hidden_hbm, hid.at[pl.ds(2, tile_rows), pl.ds(EDGE, tile_cols)]),
        (gates_hbm, gates_w),
        (cand_hbm, cand_w),
    ]
    locals_ = [
        pltpu.make_async_copy(src, dst, local_sems.at[i]) for i, (src, dst) in enumerate(locals_)
    ]
    for copy in locals_:
        copy.start()

    zeros = functools.partial(jnp.zeros, dtype=BF16)
    strips[pl.ds(0, RADIUS)] = zeros((RADIUS, LANES, channels))
    strips[pl.ds(RADIUS + height, RADIUS)] = zeros((RADIUS, LANES, channels))
    used = breadth + EDGE + HALO
    if used < LANES:
        strips[pl.ds(RADIUS, height), pl.ds(used, LANES - used)] = zeros(
            (height, LANES - used, channels)
        )

    @pl.when(lat == 0)
    def _():
        hid[pl.ds(0, 2)] = zeros((2, span, channels))
        mot[pl.ds(0, 2)] = zeros((2, span, channels))

    @pl.when(lat == last)
    def _():
        hid[pl.ds(2 + tile_rows, 2)] = zeros((2, span, channels))
        mot[pl.ds(2 + tile_rows, 2)] = zeros((2, span, channels))

    barrier = pltpu.get_barrier_semaphore()
    peers = 0
    for group in (west, lon, east):
        for other in range(lats):
            if group is lon:
                if other == 0:
                    continue
                target = lax.rem(lat + other, lats)
            else:
                target = jnp.int32(other)
            pl.semaphore_signal(
                barrier,
                inc=1,
                device_id={"lon": group, "lat": target},
                device_id_type=pl.DeviceIdType.MESH,
            )
            peers += 1
    pl.semaphore_wait(barrier, peers)

    next_lat, prev_lat = lax.rem(lat + 1, lats), lax.rem(lat + last, lats)
    next_lon = lax.rem(lon + (lat + 1) // lats, lons)
    prev_lon = lax.rem(lon + lons - (lats - lat) // lats, lons)
    seconds = (second_sends, second_recvs)
    second_copies = [
        copy_to(
            second_hbm.at[:, pl.ds(breadth - HALO, HALO)],
            strips.at[pl.ds(RADIUS, height), pl.ds(EDGE - HALO, HALO)],
            seconds,
            0,
            next_lon,
            next_lat,
        ),
        copy_to(
            second_hbm.at[:, pl.ds(0, HALO)],
            strips.at[pl.ds(RADIUS, height), pl.ds(EDGE + breadth, HALO)],
            seconds,
            1,
            prev_lon,
            prev_lat,
        ),
    ]
    for copy in second_copies:
        copy.start()

    hids = (hid_sends, hid_recvs)
    sides = []
    slot = 0
    for dy in (-1, 0, 1):
        for dx in (-1, 0, 1):
            if dy == 0 and dx == 0:
                continue
            src_rows = {-1: pl.ds(0, 2), 0: pl.ds(0, tile_rows), 1: pl.ds(tile_rows - 2, 2)}[dy]
            dst_rows = {-1: pl.ds(2 + tile_rows, 2), 0: pl.ds(2, tile_rows), 1: pl.ds(0, 2)}[dy]
            src_cols = {
                -1: pl.ds(0, HALO),
                0: pl.ds(0, tile_cols),
                1: pl.ds(tile_cols - HALO, HALO),
            }[dx]
            dst_cols = {
                -1: pl.ds(EDGE + tile_cols, HALO),
                0: pl.ds(EDGE, tile_cols),
                1: pl.ds(EDGE - HALO, HALO),
            }[dx]
            to_lon = {-1: west, 0: lon, 1: east}[dx]
            to_lat = {-1: prev_lat, 0: lat, 1: next_lat}[dy]
            copy = copy_to(
                hidden_hbm.at[src_rows, src_cols],
                hid.at[dst_rows, dst_cols],
                hids,
                slot,
                to_lon,
                to_lat,
            )
            sends = {-1: lat > 0, 0: None, 1: lat < last}[dy]
            gets = {-1: lat < last, 0: None, 1: lat > 0}[dy]
            sides.append((copy, sends, gets))
            slot += 1

    def maybe(condition, action):
        if condition is None:
            action()
        else:
            pl.when(condition)(action)

    encoder_wide[pl.ds(0, WIN * WIN)] = encoder_in[...].astype(F32)
    encoder_slots[...] = jnp.zeros(encoder_slots.shape, F32)
    for shift_y in range(WIN):
        group, place = divmod(shift_y, PER_GROUP)
        piece = encoder_wide[pl.ds(WIN * shift_y, SLOT)]
        row = lax.broadcasted_iota(jnp.int32, piece.shape, 0)
        target = pl.ds(group * LANES + SLOT * place, SLOT)
        encoder_slots[target] = jnp.where(row < WIN, piece, 0.0)
    encoder[...] = encoder_slots[...].astype(BF16)

    locals_[0].wait()

    def reverse(pair, carry):
        rows = first[pl.ds(2 * pair, 2)].reshape(2 * breadth, channels)
        rows = jnp.dot(mirror(breadth), rows, preferred_element_type=F32).astype(BF16)
        first[pl.ds(2 * pair, 2)] = rows.reshape(2, breadth, channels)
        return carry

    lax.fori_loop(0, height // 2, reverse, 0)
    locals_[1].wait()
    for copy in second_copies:
        copy.wait_recv()
    for copy, sends, gets in sides:
        maybe(sends, copy.start)

    block = tile_rows + 4
    flip = 1 - (2 * lat) // lats
    slab_cols = pl.ds(pl.multiple_of(EDGE + lat * breadth, EDGE), breadth)

    def blocks(dest):
        top = dest * tile_rows
        return [
            (dest == 0, pl.ds(top, block - 2), pl.ds(2, block - 2)),
            ((dest > 0) & (dest < last), pl.ds(top - 2, block), pl.ds(0, block)),
            (dest == last, pl.ds(top - 2, block - 2), pl.ds(0, block - 2)),
        ]

    def slab_copy(dest, source, src_rows, dst_rows):
        cols = pl.ds(pl.multiple_of(EDGE + source * breadth, EDGE), breadth)
        return pltpu.make_async_remote_copy(
            src_ref=motion.at[src_rows],
            dst_ref=mot.at[dst_rows, cols],
            send_sem=mot_sends.at[dest],
            recv_sem=mot_recvs.at[source],
            device_id={"lon": lon, "lat": dest},
            device_id_type=pl.DeviceIdType.MESH,
        )

    def own_copy(src_rows, dst_rows):
        return pltpu.make_async_copy(
            motion.at[src_rows], mot.at[dst_rows, slab_cols], mot_sends.at[lat]
        )

    def west_copy(dest, src_rows, dst_rows):
        return pltpu.make_async_remote_copy(
            src_ref=motion.at[src_rows, pl.ds(0, HALO)],
            dst_ref=mot.at[dst_rows, pl.ds(EDGE + tile_cols, HALO)],
            send_sem=rim_sends.at[dest],
            recv_sem=rim_recvs.at[0],
            device_id={"lon": west, "lat": dest},
            device_id_type=pl.DeviceIdType.MESH,
        )

    def east_copy(dest, src_rows, dst_rows):
        return pltpu.make_async_remote_copy(
            src_ref=motion.at[src_rows, pl.ds(breadth - HALO, HALO)],
            dst_ref=mot.at[dst_rows, pl.ds(EDGE - HALO, HALO)],
            send_sem=rim_sends.at[lats + dest],
            recv_sem=rim_recvs.at[1],
            device_id={"lon": east, "lat": dest},
            device_id_type=pl.DeviceIdType.MESH,
        )

    pairs = height // 2

    def step(index, carry):
        pair = flip * (pairs - 1 - index) + (1 - flip) * index
        correlate_rows(pair, first, strips, encoder, motion)
        return carry

    done = 0
    for turn in range(lats):
        upto = min(height, (turn + 1) * tile_rows + 2) // 2
        lax.fori_loop(done, upto, step, 0)
        done = upto
        dest = flip * (last - turn) + (1 - flip) * turn
        for here, src_rows, dst_rows in blocks(dest):
            maybe(here & (lat != dest), slab_copy(dest, lat, src_rows, dst_rows).start)
            maybe(here & (lat == dest), own_copy(src_rows, dst_rows).start)
            maybe(here & (lat == 0), west_copy(dest, src_rows, dst_rows).start)
            maybe(here & (lat == last), east_copy(dest, src_rows, dst_rows).start)

    locals_[2].wait()
    locals_[3].wait()
    locals_[4].wait()
    for copy, sends, gets in sides:
        maybe(gets, copy.wait_recv)

    def state_rows(pair, carry):
        fields = jnp.concatenate(stacked(hid, 2 * pair, 2), axis=1)
        for q in range(3):
            weights = gates_w[:, q, :channels].reshape(fields.shape[1], -1)
            sums = jnp.dot(fields, weights, preferred_element_type=F32)
            state_sums[q, pl.ds(2 * pair, 2)] = sums.reshape(2, span, -1)
        return carry

    lax.fori_loop(0, (tile_rows + 2) // 2, state_rows, 0)

    def columns_sum(cols_list):
        def taps(first_row, rows):
            taken = [
                [mot[pl.ds(first_row + p, rows), cols] for p in range(3)] for cols in cols_list
            ]
            flat = [
                jnp.concatenate([t.reshape(-1, channels) for t in three], axis=1)
                for three in taken
            ]
            return jnp.concatenate(flat, axis=0)

        def split(sums, rows):
            share = sums.shape[0] // len(cols_list)
            return [
                sums[i * share : (i + 1) * share].reshape(rows, share // rows, -1)
                for i in range(len(cols_list))
            ]

        fields = taps(0, tile_rows + 2)
        for q in range(3):
            weights = gates_w[:, q, channels:].reshape(fields.shape[1], -1)
            sums = jnp.dot(fields, weights, preferred_element_type=F32)
            for cols, part in zip(cols_list, split(sums, tile_rows + 2)):
                state_sums[q, :, cols] += part
        fields = taps(1, tile_rows)
        weights = jnp.concatenate(
            [cand_w[:, q, channels:].reshape(fields.shape[1], -1) for q in range(3)], axis=1
        )
        sums = jnp.dot(fields, weights, preferred_element_type=F32)
        for cols, part in zip(cols_list, split(sums, tile_rows)):
            cand_sums[:, cols] = part

    def slab_sum(turn, carry):
        half = max(lats // 2, 1)
        mine = (lat // half) * half
        other = lats - half - mine
        near = mine + lax.rem(lat + turn, half)
        far = other + lax.rem(lat + turn, half)
        beyond = turn // half
        source = near * (1 - beyond) + far * beyond
        for here, src_rows, dst_rows in blocks(lat):
            maybe(here & (turn == 0), own_copy(src_rows, dst_rows).wait)
            maybe(here & (turn > 0), slab_copy(lat, source, src_rows, dst_rows).wait_recv)
        columns_sum([pl.ds(pl.multiple_of(EDGE + source * breadth, EDGE), breadth)])
        return carry

    lax.fori_loop(0, lats - 1, slab_sum, 0)
    for here, src_rows, dst_rows in blocks(lat):
        maybe(here, west_copy(lat, src_rows, dst_rows).wait_recv)
        maybe(here, east_copy(lat, src_rows, dst_rows).wait_recv)
    columns_sum([pl.ds(0, EDGE), pl.ds(EDGE + tile_cols, EDGE)])
    lax.fori_loop(lats - 1, lats, slab_sum, 0)

    def gate_rows(line, carry):
        a, b, c = [state_sums[q, line] for q in range(3)]
        index = lax.rem(lat * tile_rows + line + height - 1, height)
        values = jax.nn.sigmoid(b + side_sum(a, c) * metric[index])
        update[line] = values[:, :channels]
        reset[line] = (values[:, channels:] * hid[line + 1].astype(F32)).astype(BF16)
        return carry

    lax.fori_loop(0, tile_rows + 2, gate_rows, 0)

    def candidate_rows(pair, carry):
        fields = jnp.concatenate(stacked(reset, 2 * pair, 2), axis=1)
        weights = jnp.concatenate(
            [cand_w[:, q, :channels].reshape(fields.shape[1], -1) for q in range(3)], axis=1
        )
        sums = jnp.dot(fields, weights, preferred_element_type=F32)
        for row in range(2):
            part = sums[row * span : (row + 1) * span] + cand_sums[2 * pair + row]
            a, b, c = [part[:, q * channels : (q + 1) * channels] for q in range(3)]
            index = lat * tile_rows + 2 * pair + row
            candidate = jnp.tanh(b + side_sum(a, c) * metric[index])
            gate = update[2 * pair + row + 1]
            state = hid[2 * pair + row + 2].astype(F32)
            new = (1.0 - gate) * state + gate * candidate
            out[2 * pair + row] = new[EDGE : EDGE + tile_cols].astype(BF16)
        return carry

    lax.fori_loop(0, tile_rows // 2, candidate_rows, 0)

    for copy in second_copies:
        copy.wait_send()
    for copy, sends, gets in sides:
        maybe(sends, copy.wait_send)
    for dest in range(lats):
        dest = jnp.int32(dest)
        for here, src_rows, dst_rows in blocks(dest):
            maybe(here & (lat != dest), slab_copy(dest, lat, src_rows, dst_rows).wait_send)
            maybe(here & (lat == 0), west_copy(dest, src_rows, dst_rows).wait_send)
            maybe(here & (lat == last), east_copy(dest, src_rows, dst_rows).wait_send)


def body(lats, lons, first, second, hidden, encoder, gates, cand, row_metric):
    height, breadth, channels = first.shape
    tile_rows, tile_cols = hidden.shape[:2]
    span = tile_cols + 2 * EDGE
    groups = -(-WIN // PER_GROUP)
    hbm = pl.BlockSpec(memory_space=pl.ANY)
    vmem = pl.BlockSpec(memory_space=pltpu.VMEM)
    dma = pltpu.SemaphoreType.DMA
    return pl.pallas_call(
        functools.partial(kernel, lats, lons),
        out_shape=jax.ShapeDtypeStruct(hidden.shape, hidden.dtype),
        in_specs=[
            pl.BlockSpec(memory_space=pltpu.SMEM),
            hbm,
            hbm,
            hbm,
            vmem,
            hbm,
            hbm,
        ],
        out_specs=vmem,
        scratch_shapes=[
            pltpu.VMEM(first.shape, BF16),
            pltpu.VMEM((height + 2 * RADIUS, LANES, channels), BF16),
            pltpu.VMEM((groups * LANES, encoder.shape[1]), BF16),
            pltpu.VMEM((groups * LANES, encoder.shape[1]), F32),
            pltpu.VMEM((groups * LANES, encoder.shape[1]), F32),
            pltpu.VMEM(gates.shape, BF16),
            pltpu.VMEM(cand.shape, BF16),
            pltpu.VMEM((height, breadth, channels), BF16),
            pltpu.VMEM((tile_rows + 4, span, channels), BF16),
            pltpu.VMEM((tile_rows + 4, span, channels), BF16),
            pltpu.VMEM((tile_rows + 2, span, channels), BF16),
            pltpu.VMEM((tile_rows + 2, span, channels), F32),
            pltpu.VMEM((3, tile_rows + 2, span, gates.shape[-1]), F32),
            pltpu.VMEM((tile_rows, span, 3 * cand.shape[-1]), F32),
            dma((5,)),
            dma((2,)),
            dma((2,)),
            dma((8,)),
            dma((8,)),
            dma((lats,)),
            dma((lats,)),
            dma((2 * lats,)),
            dma((2,)),
        ],
        compiler_params=pltpu.CompilerParams(
            collective_id=0, has_side_effects=True, vmem_limit_bytes=60 * 1024 * 1024
        ),
    )(row_metric, first, second, hidden, encoder, gates, cand)


def solution(mesh):
    return jax.shard_map(
        functools.partial(body, mesh.shape["lat"], mesh.shape["lon"]),
        mesh=mesh,
        in_specs=(
            P(None, ("lon", "lat"), None),
            P(None, ("lon", "lat"), None),
            P("lat", "lon", None),
            P(),
            P(),
            P(),
            P(),
        ),
        out_specs=P("lat", "lon", None),
        check_vma=False,
    )
```

```python
import functools

import jax
import jax.numpy as jnp
from jax import lax
from jax.experimental import pallas as pl
from jax.experimental.pallas import tpu as pltpu
from jax.sharding import PartitionSpec as P

RADIUS = 8
WIN = 2 * RADIUS + 1
EDGE = 16
HALO = 8
LANES = 128
SLOT = 24
PER_GROUP = LANES // SLOT
BF16 = jnp.bfloat16
F32 = jnp.float32


def copy_to(src, dst, sems, slot, lon, lat):
    return pltpu.make_async_remote_copy(
        src_ref=src,
        dst_ref=dst,
        send_sem=sems[0].at[slot],
        recv_sem=sems[1].at[slot],
        device_id={"lon": lon, "lat": lat},
        device_id_type=pl.DeviceIdType.MESH,
    )


def mirror(breadth):
    size = 2 * breadth
    total = lax.broadcasted_iota(jnp.int32, (size, size), 0)
    total += lax.broadcasted_iota(jnp.int32, (size, size), 1)
    return ((total == breadth - 1) | (total == 3 * breadth - 1)).astype(F32).astype(BF16)


def correlate_rows(pair, first, strips, encoder, motion):
    breadth = first.shape[1]
    left = first[pl.ds(2 * pair, 2)].reshape(2 * breadth, first.shape[2])
    groups = -(-WIN // PER_GROUP)
    packed = [[jnp.zeros((breadth, LANES), F32)] * groups for _ in range(2)]
    lane = lax.broadcasted_iota(jnp.int32, (breadth, LANES), 1)
    for step in range(0, WIN + 1, 2):
        right = strips[pl.ds(2 * pair + step, 2)].reshape(2 * LANES, first.shape[2])
        product = lax.dot_general(
            left, right, (((1,), (1,)), ((), ())), preferred_element_type=F32
        )
        for sub in range(2):
            for row in range(2):
                shift_y = step + sub - row
                if not 0 <= shift_y < WIN:
                    continue
                group, place = divmod(shift_y, PER_GROUP)
                band = product[
                    row * breadth : (row + 1) * breadth, sub * LANES : (sub + 1) * LANES
                ]
                start = SLOT * place
                turned = pltpu.roll(
                    band,
                    (start - (EDGE - RADIUS) - (breadth - 1)) % LANES,
                    1,
                    stride=1,
                    stride_axis=0,
                )
                inside = (lane >= start) & (lane < start + WIN)
                packed[row][group] = jnp.where(inside, turned, packed[row][group])
    scale = first.shape[2] ** (-0.5)
    rows = [jnp.concatenate(packed[row], axis=1) for row in range(2)]
    correlation = (jnp.concatenate(rows, axis=0) * scale).astype(BF16)
    out = jnp.dot(correlation, encoder[...], preferred_element_type=F32)
    out = jnp.maximum(out, 0.0).astype(BF16)
    out = jnp.dot(mirror(breadth), out, preferred_element_type=F32).astype(BF16)
    motion[pl.ds(2 * pair, 2)] = out.reshape(2, breadth, -1)


def side_sum(west, east):
    span = west.shape[0]
    return pltpu.roll(west, 1, 0) + pltpu.roll(east, span - 1, 0)


def stacked(field, start, rows):
    span = field.shape[1]
    parts = [field[pl.ds(start + p, rows)].reshape(rows * span, -1) for p in range(3)]
    return parts


def kernel(
    lats,
    lons,
    metric,
    first_hbm,
    second_hbm,
    hidden_hbm,
    encoder_in,
    gates_hbm,
    cand_hbm,
    out,
    first,
    strips,
    encoder,
    encoder_wide,
    encoder_slots,
    gates_w,
    cand_w,
    motion,
    hid,
    mot,
    reset,
    update,
    state_sums,
    cand_sums,
    local_sems,
    second_sends,
    second_recvs,
    hid_sends,
    hid_recvs,
    mot_sends,
    mot_recvs,
    rim_sends,
    rim_recvs,
):
    height, breadth, channels = first.shape
    tile_rows, tile_cols = out.shape[0], out.shape[1]
    span = hid.shape[1]
    lon, lat = lax.axis_index("lon"), lax.axis_index("lat")
    east, west = lax.rem(lon + 1, lons), lax.rem(lon + lons - 1, lons)
    last = lats - 1

    locals_ = [
        (first_hbm, first),
        (second_hbm, strips.at[pl.ds(RADIUS, height), pl.ds(EDGE, breadth)]),
        (hidden_hbm, hid.at[pl.ds(2, tile_rows), pl.ds(EDGE, tile_cols)]),
        (gates_hbm, gates_w),
        (cand_hbm, cand_w),
    ]
    locals_ = [
        pltpu.make_async_copy(src, dst, local_sems.at[i]) for i, (src, dst) in enumerate(locals_)
    ]
    for copy in locals_:
        copy.start()

    zeros = functools.partial(jnp.zeros, dtype=BF16)
    strips[pl.ds(0, RADIUS)] = zeros((RADIUS, LANES, channels))
    strips[pl.ds(RADIUS + height, RADIUS)] = zeros((RADIUS, LANES, channels))
    used = breadth + EDGE + HALO
    if used < LANES:
        strips[pl.ds(RADIUS, height), pl.ds(used, LANES - used)] = zeros(
            (height, LANES - used, channels)
        )

    @pl.when(lat == 0)
    def _():
        hid[pl.ds(0, 2)] = zeros((2, span, channels))
        mot[pl.ds(0, 2)] = zeros((2, span, channels))

    @pl.when(lat == last)
    def _():
        hid[pl.ds(2 + tile_rows, 2)] = zeros((2, span, channels))
        mot[pl.ds(2 + tile_rows, 2)] = zeros((2, span, channels))

    barrier = pltpu.get_barrier_semaphore()
    peers = 0
    for group in (west, lon, east):
        for other in range(lats):
            if group is lon:
                if other == 0:
                    continue
                target = lax.rem(lat + other, lats)
            else:
                target = jnp.int32(other)
            pl.semaphore_signal(
                barrier,
                inc=1,
                device_id={"lon": group, "lat": target},
                device_id_type=pl.DeviceIdType.MESH,
            )
            peers += 1
    pl.semaphore_wait(barrier, peers)

    next_lat, prev_lat = lax.rem(lat + 1, lats), lax.rem(lat + last, lats)
    next_lon = lax.rem(lon + (lat + 1) // lats, lons)
    prev_lon = lax.rem(lon + lons - (lats - lat) // lats, lons)
    seconds = (second_sends, second_recvs)
    second_copies = [
        copy_to(
            second_hbm.at[:, pl.ds(breadth - HALO, HALO)],
            strips.at[pl.ds(RADIUS, height), pl.ds(EDGE - HALO, HALO)],
            seconds,
            0,
            next_lon,
            next_lat,
        ),
        copy_to(
            second_hbm.at[:, pl.ds(0, HALO)],
            strips.at[pl.ds(RADIUS, height), pl.ds(EDGE + breadth, HALO)],
            seconds,
            1,
            prev_lon,
            prev_lat,
        ),
    ]
    for copy in second_copies:
        copy.start()

    hids = (hid_sends, hid_recvs)
    sides = []
    slot = 0
    for dy in (-1, 0, 1):
        for dx in (-1, 0, 1):
            if dy == 0 and dx == 0:
                continue
            src_rows = {-1: pl.ds(0, 2), 0: pl.ds(0, tile_rows), 1: pl.ds(tile_rows - 2, 2)}[dy]
            dst_rows = {-1: pl.ds(2 + tile_rows, 2), 0: pl.ds(2, tile_rows), 1: pl.ds(0, 2)}[dy]
            src_cols = {
                -1: pl.ds(0, HALO),
                0: pl.ds(0, tile_cols),
                1: pl.ds(tile_cols - HALO, HALO),
            }[dx]
            dst_cols = {
                -1: pl.ds(EDGE + tile_cols, HALO),
                0: pl.ds(EDGE, tile_cols),
                1: pl.ds(EDGE - HALO, HALO),
            }[dx]
            to_lon = {-1: west, 0: lon, 1: east}[dx]
            to_lat = {-1: prev_lat, 0: lat, 1: next_lat}[dy]
            copy = copy_to(
                hidden_hbm.at[src_rows, src_cols],
                hid.at[dst_rows, dst_cols],
                hids,
                slot,
                to_lon,
                to_lat,
            )
            sends = {-1: lat > 0, 0: None, 1: lat < last}[dy]
            gets = {-1: lat < last, 0: None, 1: lat > 0}[dy]
            sides.append((copy, sends, gets))
            slot += 1

    def maybe(condition, action):
        if condition is None:
            action()
        else:
            pl.when(condition)(action)

    encoder_wide[pl.ds(0, WIN * WIN)] = encoder_in[...].astype(F32)
    encoder_slots[...] = jnp.zeros(encoder_slots.shape, F32)
    for shift_y in range(WIN):
        group, place = divmod(shift_y, PER_GROUP)
        piece = encoder_wide[pl.ds(WIN * shift_y, SLOT)]
        row = lax.broadcasted_iota(jnp.int32, piece.shape, 0)
        target = pl.ds(group * LANES + SLOT * place, SLOT)
        encoder_slots[target] = jnp.where(row < WIN, piece, 0.0)
    encoder[...] = encoder_slots[...].astype(BF16)

    locals_[0].wait()

    def reverse(pair, carry):
        rows = first[pl.ds(2 * pair, 2)].reshape(2 * breadth, channels)
        rows = jnp.dot(mirror(breadth), rows, preferred_element_type=F32).astype(BF16)
        first[pl.ds(2 * pair, 2)] = rows.reshape(2, breadth, channels)
        return carry

    lax.fori_loop(0, height // 2, reverse, 0)
    locals_[1].wait()
    for copy in second_copies:
        copy.wait_recv()
    for copy, sends, gets in sides:
        maybe(sends, copy.start)

    block = tile_rows + 4
    flip = 1 - (2 * lat) // lats
    slab_cols = pl.ds(pl.multiple_of(EDGE + lat * breadth, EDGE), breadth)

    def blocks(dest):
        top = dest * tile_rows
        return [
            (dest == 0, pl.ds(top, block - 2), pl.ds(2, block - 2)),
            ((dest > 0) & (dest < last), pl.ds(top - 2, block), pl.ds(0, block)),
            (dest == last, pl.ds(top - 2, block - 2), pl.ds(0, block - 2)),
        ]

    half_block = block // 2

    def pieces(dest, part):
        rim = ((dest == 0) & (part == 0)) | ((dest == last) & (part == 1))
        kept = half_block - 2
        top = dest * tile_rows
        return [
            (rim, pl.ds(top + kept * part, kept), pl.ds(2 + kept * part, kept)),
            (
                jnp.logical_not(rim),
                pl.ds(top - 2 + half_block * part, half_block),
                pl.ds(half_block * part, half_block),
            ),
        ]

    def slab_copy(dest, source, part, src_rows, dst_rows):
        cols = pl.ds(pl.multiple_of(EDGE + source * breadth, EDGE), breadth)
        return pltpu.make_async_remote_copy(
            src_ref=motion.at[src_rows],
            dst_ref=mot.at[dst_rows, cols],
            send_sem=mot_sends.at[2 * dest + part],
            recv_sem=mot_recvs.at[2 * source + part],
            device_id={"lon": lon, "lat": dest},
            device_id_type=pl.DeviceIdType.MESH,
        )

    def own_copy(src_rows, dst_rows):
        return pltpu.make_async_copy(
            motion.at[src_rows], mot.at[dst_rows, slab_cols], mot_sends.at[2 * lat]
        )

    def west_copy(dest, src_rows, dst_rows):
        return pltpu.make_async_remote_copy(
            src_ref=motion.at[src_rows, pl.ds(0, HALO)],
            dst_ref=mot.at[dst_rows, pl.ds(EDGE + tile_cols, HALO)],
            send_sem=rim_sends.at[dest],
            recv_sem=rim_recvs.at[0],
            device_id={"lon": west, "lat": dest},
            device_id_type=pl.DeviceIdType.MESH,
        )

    def east_copy(dest, src_rows, dst_rows):
        return pltpu.make_async_remote_copy(
            src_ref=motion.at[src_rows, pl.ds(breadth - HALO, HALO)],
            dst_ref=mot.at[dst_rows, pl.ds(EDGE - HALO, HALO)],
            send_sem=rim_sends.at[lats + dest],
            recv_sem=rim_recvs.at[1],
            device_id={"lon": east, "lat": dest},
            device_id_type=pl.DeviceIdType.MESH,
        )

    pairs = height // 2

    def step(index, carry):
        pair = flip * (pairs - 1 - index) + (1 - flip) * index
        correlate_rows(pair, first, strips, encoder, motion)
        return carry

    done = 0
    for turn in range(lats):
        dest = flip * (last - turn) + (1 - flip) * turn
        for order, ready in enumerate(
            (turn * tile_rows + half_block - 2, (turn + 1) * tile_rows + 2)
        ):
            upto = min(pairs, (ready + 1) // 2)
            lax.fori_loop(done, upto, step, 0)
            done = upto
            part = flip * (1 - order) + (1 - flip) * order
            for here, src_rows, dst_rows in pieces(dest, part):
                copy = slab_copy(dest, lat, part, src_rows, dst_rows)
                maybe(here & (lat != dest), copy.start)
        for here, src_rows, dst_rows in blocks(dest):
            maybe(here & (lat == dest), own_copy(src_rows, dst_rows).start)
            maybe(here & (lat == 0), west_copy(dest, src_rows, dst_rows).start)
            maybe(here & (lat == last), east_copy(dest, src_rows, dst_rows).start)

    locals_[2].wait()
    locals_[3].wait()
    locals_[4].wait()
    for copy, sends, gets in sides:
        maybe(gets, copy.wait_recv)

    def state_rows(pair, carry):
        fields = jnp.concatenate(stacked(hid, 2 * pair, 2), axis=1)
        for q in range(3):
            weights = gates_w[:, q, :channels].reshape(fields.shape[1], -1)
            sums = jnp.dot(fields, weights, preferred_element_type=F32)
            state_sums[q, pl.ds(2 * pair, 2)] = sums.reshape(2, span, -1)
        return carry

    lax.fori_loop(0, (tile_rows + 2) // 2, state_rows, 0)

    def columns_sum(cols_list):
        def taps(first_row, rows):
            taken = [
                [mot[pl.ds(first_row + p, rows), cols] for p in range(3)] for cols in cols_list
            ]
            flat = [
                jnp.concatenate([t.reshape(-1, channels) for t in three], axis=1)
                for three in taken
            ]
            return jnp.concatenate(flat, axis=0)

        def split(sums, rows):
            share = sums.shape[0] // len(cols_list)
            return [
                sums[i * share : (i + 1) * share].reshape(rows, share // rows, -1)
                for i in range(len(cols_list))
            ]

        fields = taps(0, tile_rows + 2)
        for q in range(3):
            weights = gates_w[:, q, channels:].reshape(fields.shape[1], -1)
            sums = jnp.dot(fields, weights, preferred_element_type=F32)
            for cols, part in zip(cols_list, split(sums, tile_rows + 2)):
                state_sums[q, :, cols] += part
        fields = taps(1, tile_rows)
        weights = jnp.concatenate(
            [cand_w[:, q, channels:].reshape(fields.shape[1], -1) for q in range(3)], axis=1
        )
        sums = jnp.dot(fields, weights, preferred_element_type=F32)
        for cols, part in zip(cols_list, split(sums, tile_rows)):
            cand_sums[:, cols] = part

    def slab_sum(turn, carry):
        half = max(lats // 2, 1)
        mine = (lat // half) * half
        other = lats - half - mine
        near = mine + lax.rem(lat + turn, half)
        far = other + lax.rem(lat + turn, half)
        beyond = turn // half
        source = near * (1 - beyond) + far * beyond
        for here, src_rows, dst_rows in blocks(lat):
            maybe(here & (turn == 0), own_copy(src_rows, dst_rows).wait)
        for part in range(2):
            for here, src_rows, dst_rows in pieces(lat, part):
                copy = slab_copy(lat, source, part, src_rows, dst_rows)
                maybe(here & (turn > 0), copy.wait_recv)
        columns_sum([pl.ds(pl.multiple_of(EDGE + source * breadth, EDGE), breadth)])
        return carry

    lax.fori_loop(0, lats - 1, slab_sum, 0)
    for here, src_rows, dst_rows in blocks(lat):
        maybe(here, west_copy(lat, src_rows, dst_rows).wait_recv)
        maybe(here, east_copy(lat, src_rows, dst_rows).wait_recv)
    columns_sum([pl.ds(0, EDGE), pl.ds(EDGE + tile_cols, EDGE)])
    lax.fori_loop(lats - 1, lats, slab_sum, 0)

    def gate_rows(line, carry):
        a, b, c = [state_sums[q, line] for q in range(3)]
        index = lax.rem(lat * tile_rows + line + height - 1, height)
        values = 0.5 + 0.5 * jnp.tanh(0.5 * (b + side_sum(a, c) * metric[index]))
        update[line] = values[:, :channels]
        reset[line] = (values[:, channels:] * hid[line + 1].astype(F32)).astype(BF16)
        return carry

    lax.fori_loop(0, tile_rows + 2, gate_rows, 0)

    def candidate_rows(pair, carry):
        fields = jnp.concatenate(stacked(reset, 2 * pair, 2), axis=1)
        weights = jnp.concatenate(
            [cand_w[:, q, :channels].reshape(fields.shape[1], -1) for q in range(3)], axis=1
        )
        sums = jnp.dot(fields, weights, preferred_element_type=F32)
        for row in range(2):
            part = sums[row * span : (row + 1) * span] + cand_sums[2 * pair + row]
            a, b, c = [part[:, q * channels : (q + 1) * channels] for q in range(3)]
            index = lat * tile_rows + 2 * pair + row
            candidate = jnp.tanh(b + side_sum(a, c) * metric[index])
            gate = update[2 * pair + row + 1]
            state = hid[2 * pair + row + 2].astype(F32)
            new = (1.0 - gate) * state + gate * candidate
            out[2 * pair + row] = new[EDGE : EDGE + tile_cols].astype(BF16)
        return carry

    lax.fori_loop(0, tile_rows // 2, candidate_rows, 0)

    for copy in second_copies:
        copy.wait_send()
    for copy, sends, gets in sides:
        maybe(sends, copy.wait_send)
    for dest in range(lats):
        dest = jnp.int32(dest)
        for part in range(2):
            for here, src_rows, dst_rows in pieces(dest, part):
                copy = slab_copy(dest, lat, part, src_rows, dst_rows)
                maybe(here & (lat != dest), copy.wait_send)
        for here, src_rows, dst_rows in blocks(dest):
            maybe(here & (lat == 0), west_copy(dest, src_rows, dst_rows).wait_send)
            maybe(here & (lat == last), east_copy(dest, src_rows, dst_rows).wait_send)


def body(lats, lons, first, second, hidden, encoder, gates, cand, row_metric):
    height, breadth, channels = first.shape
    tile_rows, tile_cols = hidden.shape[:2]
    span = tile_cols + 2 * EDGE
    groups = -(-WIN // PER_GROUP)
    hbm = pl.BlockSpec(memory_space=pl.ANY)
    vmem = pl.BlockSpec(memory_space=pltpu.VMEM)
    dma = pltpu.SemaphoreType.DMA
    return pl.pallas_call(
        functools.partial(kernel, lats, lons),
        out_shape=jax.ShapeDtypeStruct(hidden.shape, hidden.dtype),
        in_specs=[
            pl.BlockSpec(memory_space=pltpu.SMEM),
            hbm,
            hbm,
            hbm,
            vmem,
            hbm,
            hbm,
        ],
        out_specs=vmem,
        scratch_shapes=[
            pltpu.VMEM(first.shape, BF16),
            pltpu.VMEM((height + 2 * RADIUS, LANES, channels), BF16),
            pltpu.VMEM((groups * LANES, encoder.shape[1]), BF16),
            pltpu.VMEM((groups * LANES, encoder.shape[1]), F32),
            pltpu.VMEM((groups * LANES, encoder.shape[1]), F32),
            pltpu.VMEM(gates.shape, BF16),
            pltpu.VMEM(cand.shape, BF16),
            pltpu.VMEM((height, breadth, channels), BF16),
            pltpu.VMEM((tile_rows + 4, span, channels), BF16),
            pltpu.VMEM((tile_rows + 4, span, channels), BF16),
            pltpu.VMEM((tile_rows + 2, span, channels), BF16),
            pltpu.VMEM((tile_rows + 2, span, channels), F32),
            pltpu.VMEM((3, tile_rows + 2, span, gates.shape[-1]), F32),
            pltpu.VMEM((tile_rows, span, 3 * cand.shape[-1]), F32),
            dma((5,)),
            dma((2,)),
            dma((2,)),
            dma((8,)),
            dma((8,)),
            dma((2 * lats,)),
            dma((2 * lats,)),
            dma((2 * lats,)),
            dma((2,)),
        ],
        compiler_params=pltpu.CompilerParams(
            collective_id=0, has_side_effects=True, vmem_limit_bytes=60 * 1024 * 1024
        ),
    )(row_metric, first, second, hidden, encoder, gates, cand)


def solution(mesh):
    return jax.shard_map(
        functools.partial(body, mesh.shape["lat"], mesh.shape["lon"]),
        mesh=mesh,
        in_specs=(
            P(None, ("lon", "lat"), None),
            P(None, ("lon", "lat"), None),
            P("lat", "lon", None),
            P(),
            P(),
            P(),
            P(),
        ),
        out_specs=P("lat", "lon", None),
        check_vma=False,
    )
```
